256 devices in a mesh: seq: 64 (over z, y, core), head: 4 (over x).
Axes of the slice: x: 4, y: 4, z: 8, core: 2. Of those that a mesh axis runs over, the one named last changes fastest.
Arguments:
- queries: bfloat16 [32, 64, 128], P(None, 'head'), may hold values from -12 to 12
- keys: bfloat16 [32, 8, 8192, 128], P(None, 'head', 'seq'), may hold values from -6 to 6
- values: bfloat16 [32, 8, 8192, 128], P(None, 'head', 'seq'), may hold values from -6 to 6
- codes: int32 [32, 8, 32, 8192], P(None, 'head', None, 'seq'), may hold values from 0 to 255
- centroids: float32 [8, 4, 32, 256], P('head'), may hold values from -6 to 6
- picks: int32 [32, 8, 64], P(None, 'head'), may hold values from 0 to 511, as said below
- block_len: int32 [32, 512], P(None, 'seq'), may hold values from 1 to 16
- out_weight: bfloat16 [8192, 8192], P('head', 'seq'), may hold values from -0.0625 to 0.0625
Outputs:
- estimates: float32 [32, 8, 512], P(None, 'head', 'seq')
- attended: bfloat16 [64, 4, 1024], P('seq', 'head')
- layer_out: bfloat16 [32, 8192], P('head', 'seq')
The draws below stay inside these ranges and needn't reach their ends.
Inputs may be any that keep to these rules, and one draw needn't show every extreme that they name: Each row picks[b, h, :] holds 64 different block numbers in no particular order; among the 8 blocks j * 8 to (j + 1) * 8 - 1 of any j at most 4 are picked, and in every row some j has exactly 4.
All inputs are finite; a program needn't handle non-finite values.
Results may differ from the reference program's by a relative error of at most 0.0049.
Values may be sent and summed in bfloat16 or wider, within the bound.
A program may use at most 64 MiB of HBM per device.

```python
import jax
import jax.numpy as jnp
from jax import lax

D = 8192
QH = 64
KVH = 8
HD = 128
M = 32
CENT = 256
BLK = 16
NBLK_DEV = 8
SUB = 4
KVH_DEV = 2
B = 32
NBLK = 512
S = 8192
TOPK = 64


def draw_queries(key, part):
    own = jax.random.fold_in(key, 11)
    base = 3.0 * jax.random.normal(own, (B, QH, HD), jnp.float32)
    return jnp.clip(base, -12.0, 12.0).astype(jnp.bfloat16)


def draw_keys(key, part):
    own = jax.random.fold_in(key, 12)
    base = jax.random.normal(own, (B, KVH, S, HD), jnp.float32)
    return jnp.clip(base, -6.0, 6.0).astype(jnp.bfloat16)


def draw_centroids(key, part):
    own = jax.random.fold_in(key, 14)
    base = jax.random.normal(own, (KVH, SUB, M, CENT), jnp.float32)
    return jnp.clip(base, -6.0, 6.0).astype(jnp.float32)


def pair_picks(key):
    shards = NBLK // NBLK_DEV
    base_count = NBLK_DEV // 8
    most = NBLK_DEV // 2
    key_hot, key_force, key_move, key_rank, key_order = jax.random.split(key, 5)
    places = jnp.arange(shards, dtype=jnp.int32)
    hot = jax.random.randint(key_hot, (), 0, shards).astype(jnp.int32)
    counts = jnp.full((shards,), base_count, jnp.int32)

    def force(step, counts):
        order = jax.random.permutation(jax.random.fold_in(key_force, step), shards).astype(jnp.int32) + 1
        score = jnp.where((counts > 0) & (places != hot), order, 0)
        source = jnp.argmax(score)
        return counts.at[source].add(-1).at[hot].add(1)
    counts = lax.fori_loop(0, most - base_count, force, counts)

    def move(step, counts):
        key_a, key_b, key_c = jax.random.split(jax.random.fold_in(key_move, step), 3)
        order = jax.random.permutation(key_a, shards).astype(jnp.int32) + 1
        score = jnp.where((counts > 0) & (places != hot), order, 0)
        source = jnp.argmax(score).astype(jnp.int32)
        first = jax.random.randint(key_b, (), 0, shards).astype(jnp.int32)
        second = jax.random.randint(key_c, (), 0, shards).astype(jnp.int32)
        target = shards - 1 - first * second // shards
        allowed = ((counts[target] < most) & (target != source) & (target != hot)).astype(jnp.int32)
        return counts.at[source].add(-allowed).at[target].add(allowed)
    counts = lax.fori_loop(0, 4 * TOPK, move, counts)
    ranks = jax.vmap(lambda k: jax.random.permutation(k, NBLK_DEV).astype(jnp.int32))(jax.random.split(key_rank, shards))
    chosen = (ranks < counts[:, None]).reshape(NBLK).astype(jnp.int32)
    ordered = jnp.argsort(1 - chosen, stable=True)[:TOPK].astype(jnp.int32)
    mixing = jax.random.permutation(key_order, TOPK).astype(jnp.int32)
    return ordered[mixing]


def draw_picks(key, part):
    pair_keys = jax.random.split(jax.random.fold_in(key, 13), B * KVH)
    return jax.vmap(pair_picks)(pair_keys).reshape(B, KVH, TOPK).astype(jnp.int32)


def touch_ends(result, own_key, smallest, largest):
    spot = [jax.random.randint(jax.random.fold_in(own_key, axis), (), 0, length) for axis, length in enumerate(result.shape)]
    longest = result.shape.index(max(result.shape))
    neighbour = spot[:longest] + [(spot[longest] + 1) % result.shape[longest]] + spot[longest + 1:]
    return result.at[tuple(spot)].set(smallest).at[tuple(neighbour)].set(largest)


def levels(stream_key, extent, pieces, low, high):
    def one(position, blocks):
        steps = jax.random.uniform(jax.random.fold_in(jax.random.fold_in(stream_key, 6), position), (blocks,), jnp.float32, low / len(pieces), high / len(pieces))
        return jnp.repeat(jnp.exp(steps), extent[position] // blocks).reshape((-1,) + (1,) * (len(extent) - position - 1))

    factor_of = one(*pieces[0])
    for cut in pieces[1:]:
        factor_of = factor_of * one(*cut)
    return factor_of


def gaussian(rng, extent, scale, reach, cuts=(), kind=jnp.bfloat16):
    array = scale * jax.random.normal(rng, extent, jnp.float32)
    if cuts:
        array = array * levels(rng, extent, cuts, -0.22, 0.18)
    return jnp.clip(array, -reach, reach).astype(kind)


def setup_inputs(seed: int = 0) -> dict:
    arg_keys = jax.random.split(jax.random.key(seed), 9)
    return {
        "queries": draw_queries(jax.random.fold_in(arg_keys[8], 71), 0),
        "keys": draw_keys(jax.random.fold_in(arg_keys[8], 71), 0),
        "values": gaussian(arg_keys[2], (B, KVH, S, HD), 1.0, 6.0, ((1, 4), (2, 64))),
        "codes": touch_ends(jax.random.randint(arg_keys[3], (B, KVH, M, S), 0, CENT), jax.random.fold_in(arg_keys[3], 1), 0, CENT - 1).astype(jnp.int32),
        "centroids": draw_centroids(jax.random.fold_in(arg_keys[8], 71), 0),
        "picks": draw_picks(jax.random.fold_in(arg_keys[8], 71), 0),
        "block_len": touch_ends(jax.random.randint(arg_keys[6], (B, NBLK), 1, BLK + 1), jax.random.fold_in(arg_keys[6], 1), 1, BLK).astype(jnp.int32),
        "out_weight": gaussian(arg_keys[7], (QH * HD, D), (QH * HD) ** -0.5, 0.0625, ((0, 4), (1, 64))),
    }


NEG = -1.0e30


def reference(queries, keys, values, codes, centroids, picks, block_len, out_weight):
    group = QH // KVH
    sub = HD // M
    scale = HD ** -0.5
    query_float = queries.astype(jnp.float32).reshape(B, KVH, group, M, sub)
    table = (jnp.einsum('bhgms,hsmc->bhgmc', query_float, centroids, precision=lax.Precision.HIGHEST) * scale).astype(jnp.bfloat16)

    def estimate_pair(index):
        request = index // KVH
        kv_head = index % KVH
        tab = table[request, kv_head].astype(jnp.float32)
        code = codes[request, kv_head]
        looked = jnp.take_along_axis(tab, jnp.broadcast_to(code[None], (group, M, S)), axis=2)
        approx = jnp.sum(looked, axis=1).reshape(group, NBLK, BLK)
        lens = block_len[request]
        live = (jnp.arange(BLK, dtype=jnp.int32)[None, :] < lens[:, None])[None]
        top = jnp.max(jnp.where(live, approx, NEG), axis=(0, 2))
        mass = jnp.sum(jnp.where(live, jnp.exp(approx - top[None, :, None]), 0.0), axis=(0, 2))
        return top + jnp.log(mass)

    estimates = lax.map(estimate_pair, jnp.arange(B * KVH, dtype=jnp.int32)).reshape(B, KVH, NBLK)

    def attend_pair(index):
        request = index // KVH
        kv_head = index % KVH
        chosen = picks[request, kv_head]
        token_ids = (chosen[:, None] * BLK + jnp.arange(BLK, dtype=jnp.int32)[None, :]).reshape(-1).astype(jnp.int32)
        chosen_keys = keys[request, kv_head][token_ids].astype(jnp.float32)
        chosen_values = values[request, kv_head][token_ids].astype(jnp.float32)
        lens = block_len[request][chosen]
        live = (jnp.arange(BLK, dtype=jnp.int32)[None, :] < lens[:, None]).reshape(1, -1)
        query = lax.dynamic_slice_in_dim(queries[request], kv_head * group, group, 0).astype(jnp.float32)
        score = jnp.dot(query, chosen_keys.T, precision=lax.Precision.HIGHEST) * scale
        top = jnp.max(jnp.where(live, score, NEG), axis=1)
        weight = jnp.where(live, jnp.exp(score - top[:, None]), 0.0)
        total = jnp.sum(weight, axis=1)
        acc = jnp.dot(weight, chosen_values, precision=lax.Precision.HIGHEST)
        return (acc / total[:, None]).astype(jnp.bfloat16).reshape(group * HD)

    head_out = lax.map(attend_pair, jnp.arange(B * KVH, dtype=jnp.int32)).reshape(B, KVH, group * HD)
    attended = head_out.reshape(B, KVH // KVH_DEV, KVH_DEV, group * HD).transpose(0, 2, 1, 3).reshape(B * KVH_DEV, KVH // KVH_DEV, group * HD)
    layer_out = jnp.dot(head_out.reshape(B, QH * HD), out_weight, preferred_element_type=jnp.float32).astype(jnp.bfloat16)
    return estimates, attended, layer_out
```

```python
import functools

import jax
import jax.numpy as jnp
from jax import lax
from jax.experimental import pallas as pl
from jax.experimental.pallas import tpu as pltpu
from jax.sharding import PartitionSpec as P

MESH = pl.DeviceIdType.MESH
NEG = -1e30
LIVE = -5e29
F32 = jnp.float32
BF16 = jnp.bfloat16
SCALE = 128 ** -0.5


def iota(shape, axis):
    return lax.broadcasted_iota(jnp.int32, shape, axis)


def lane_reduce(x, lane, op):
    for s in (1, 2, 4, 8):
        up = pltpu.roll(x, s, 1)
        down = pltpu.roll(x, 128 - s, 1)
        x = op(x, jnp.where((lane & s) != 0, up, down))
    return x


def kernel(
    q_hbm, k_hbm, v_hbm, codes_hbm, cent_hbm, picks_hbm, len_hbm, w_hbm,
    est_ref, att_ref, lay_ref,
    q, k, v, codes, cent, picks, lens, w,
    bias, valid, q2, acc, send1, recv1, send2, recv2, gath, g32, part, recv5,
    in_sem, k_sem, v_sem, s1, r1, s2, r2, s3, r3, s4, r4, s5, r5,
):
    seq = lax.axis_index("seq")
    x = lax.axis_index("head")
    z = seq // 8
    i = lax.rem(seq, 8)

    def local(src, dst, n):
        return pltpu.make_async_copy(src, dst, in_sem.at[n])

    loads = [
        local(picks_hbm, picks, 0), local(len_hbm, lens, 1), local(q_hbm, q, 2),
        local(codes_hbm, codes, 3), local(cent_hbm, cent, 4), local(w_hbm, w, 5),
    ]
    for c in loads[:3]:
        c.start()

    def order(t):
        return 4 + ((t + 1) // 2) * (1 - 2 * lax.rem(t, 2))

    def kv_copies(t):
        j = lax.rem(i + order(t), 8)
        y_, h_ = j // 2, lax.rem(j, 2)
        return (
            pltpu.make_async_copy(k_hbm.at[:, y_, h_], k.at[t], k_sem.at[t]),
            pltpu.make_async_copy(v_hbm.at[:, y_, h_], v.at[t], v_sem.at[t]),
        )

    def kv_start(t, carry):
        for c in kv_copies(t):
            c.start()
        return carry

    lax.fori_loop(0, 8, kv_start, 0)
    for c in loads[3:]:
        c.start()

    barrier = pltpu.get_barrier_semaphore()
    for n in range(1, 8):
        pl.semaphore_signal(barrier, inc=1, device_id=(z * 8 + lax.rem(i + n, 8), x), device_id_type=MESH)
        pl.semaphore_signal(barrier, inc=1, device_id=(lax.rem(z + n, 8) * 8 + i, x), device_id_type=MESH)
    for n in range(1, 4):
        pl.semaphore_signal(barrier, inc=1, device_id=(seq, lax.rem(x + n, 4)), device_id_type=MESH)

    lane = iota((8, 128), 1)
    block_of = iota((32, 128), 1) // 16

    loads[0].wait()
    loads[1].wait()
    spread = jnp.where(iota((8, 128), 1) // 16 == iota((8, 128), 0), 1.0, 0.0)
    len_rows = lens[...].astype(F32).T
    len_lane = jnp.dot(len_rows, spread, preferred_element_type=F32)
    place = (iota((32, 128), 1) & 15).astype(F32)
    is_valid = place < len_lane
    valid[...] = jnp.where(is_valid, 0.0, NEG)
    for h in range(2):
        near = picks[pl.ds(h, 32, stride=2), :] - seq * 8
        chosen = jnp.zeros((32, 128), F32)
        for j in range(8):
            hit = jnp.max(jnp.where(near == j, 1.0, 0.0), axis=1, keepdims=True)
            chosen = jnp.where(block_of == j, hit, chosen)
        bias[h] = jnp.where(is_valid & (chosen > 0.5), 0.0, NEG)

    loads[2].wait()

    def bundle(t, j):
        y_, h_ = j // 2, lax.rem(j, 2)
        for c in kv_copies(t):
            c.wait()
        off = bias[h_, pl.ds(y_, 8, stride=4), :]
        stat = jnp.zeros((8, 128), F32)
        for n in range(8):
            s = lax.dot_general(
                q[n * 4 + y_, h_], k[t, n], (((1,), (1,)), ((), ())), preferred_element_type=F32
            ) * SCALE + off[n : n + 1]
            top = jnp.max(s, axis=1, keepdims=True).astype(BF16).astype(F32)
            weight = jnp.where(s > LIVE, jnp.exp(s - top), 0.0)
            total = jnp.sum(weight, axis=1, keepdims=True)
            total_hi = total.astype(BF16).astype(F32)
            part_sum = jnp.dot(weight.astype(BF16), v[t, n], preferred_element_type=F32)
            send1[j, n] = part_sum.astype(BF16)
            stat = jnp.where(lane == n, top, stat)
            stat = jnp.where(lane == 16 + n, total_hi, stat)
            stat = jnp.where(lane == 32 + n, total - total_hi, stat)
        send1[j, 8] = stat.astype(BF16)

    def copy1(n):
        j = lax.rem(i + n, 8)
        return pltpu.make_async_remote_copy(
            send1.at[j], recv1.at[n], s1.at[n], r1.at[n], device_id=(z * 8 + j, x), device_id_type=MESH
        )

    pl.semaphore_wait(barrier, 17)

    def send_bundle(t, carry):
        n = order(t)
        bundle(t, lax.rem(i + n, 8))
        copy1(n).start()
        return carry

    lax.fori_loop(0, 7, send_bundle, 0)
    bundle(7, i)

    loads[3].wait()
    loads[4].wait()
    for h in range(2):
        q2[h] = q[:, h].reshape(256, 128)

    def table_step(h, m):
        row = iota((16, 256), 0) & 3
        pattern = jnp.broadcast_to(cent[h, 3, pl.ds(m, 1), :], (16, 256))
        for s in range(3):
            pattern = jnp.where(row == s, cent[h, s, pl.ds(m, 1), :], pattern)
        pattern = pattern * SCALE
        hi = pattern.astype(BF16)
        lo = (pattern - hi.astype(F32)).astype(BF16)
        own = jnp.where(iota((16, 128), 1) // 4 == m, 1.0, 0.0).astype(BF16)
        lhs = q2[h] * jnp.concatenate([own] * 16, axis=0)
        rhs = jnp.concatenate([hi] * 8 + [lo] * 8, axis=0)
        table = jnp.dot(jnp.concatenate([lhs, lhs], axis=1), rhs, preferred_element_type=F32)
        for b in range(32):
            code = jnp.broadcast_to(codes[b, h, pl.ds(m, 1), :], (8, 128))
            index = code & 127
            rows = table[b * 8 : b * 8 + 8]
            first = jnp.take_along_axis(rows[:, :128], index, axis=1, mode="promise_in_bounds")
            second = jnp.take_along_axis(rows[:, 128:], index, axis=1, mode="promise_in_bounds")
            acc[pl.ds((h * 32 + b) * 8, 8), :] += jnp.where(code > 127, second, first)

    def estimate(h, low, high):
        def step(m, carry):
            table_step(h, m)
            return carry

        lax.fori_loop(low, high, step, 0)

    def finish_estimates(h):
        rows = []
        for bb in range(4):
            base = (h * 32 + bb * 8) * 8
            off = valid[bb * 8 : bb * 8 + 8, :]
            parts = [acc[pl.ds(base + g, 8, stride=8), :] + off for g in range(8)]
            top = functools.reduce(jnp.maximum, parts)
            top = lane_reduce(top, lane, jnp.maximum)
            mass = functools.reduce(jnp.add, [jnp.where(off == 0.0, jnp.exp(a - top), 0.0) for a in parts])
            mass = lane_reduce(mass, lane, jnp.add)
            rows.append(top + jnp.log(mass))
        rows = jnp.concatenate(rows, axis=0)
        pick = jnp.where(iota((8, 128), 1) == iota((8, 128), 0) * 16, 1.0, 0.0)
        est_ref[h] = lax.dot_general(
            pick, rows, (((1,), (1,)), ((), ())), precision=lax.Precision.HIGHEST, preferred_element_type=F32
        )

    def zero(n, carry):
        acc[pl.ds(pl.multiple_of(n * 32, 32), 32), :] = jnp.zeros((32, 128), F32)
        return carry

    lax.fori_loop(0, 16, zero, 0)
    estimate(0, 0, 20)

    def merge(stats):
        top = functools.reduce(jnp.maximum, stats)
        scales = [jnp.exp(a - top) for a in stats]
        totals = [
            (pltpu.roll(a, 112, 1) + pltpu.roll(a, 96, 1)) * e for a, e in zip(stats, scales)
        ]
        return top, scales, functools.reduce(jnp.add, totals)

    for n in range(1, 8):
        copy1(n).wait_recv()
    sources = [send1.at[i]] + [recv1.at[n] for n in range(1, 8)]
    top, scales, total = merge([a[8].astype(F32) for a in sources])
    total_hi = total.astype(BF16).astype(F32)
    stat = jnp.where(lane < 8, top, jnp.where(
        lane < 32, pltpu.roll(total_hi, 16, 1), pltpu.roll(total - total_hi, 32, 1)))
    stat = stat.astype(BF16)
    for n in range(8):
        summed = functools.reduce(
            jnp.add, [e[:, n : n + 1] * a[n].astype(F32) for a, e in zip(sources, scales)]
        )
        send2[n, 0] = summed.astype(BF16)
        send2[n, 1] = stat

    def copy2(n):
        to = lax.rem(z + n, 8)
        return pltpu.make_async_remote_copy(
            send2.at[to], recv2.at[n], s2.at[n], r2.at[n], device_id=(to * 8 + i, x), device_id_type=MESH
        )

    for n in (4, 3, 5, 2, 6, 1, 7):
        copy2(n).start()
    estimate(0, 20, 32)
    estimate(1, 0, 8)

    for n in range(1, 8):
        copy2(n).wait_recv()
    sources = [send2.at[z]] + [recv2.at[n] for n in range(1, 8)]
    top, scales, total = merge([a[1].astype(F32) for a in sources])
    back = lax.rem(128 - z, 128)
    summed = functools.reduce(
        jnp.add, [pltpu.roll(e, back, 1)[:, 0:1] * a[0].astype(F32) for a, e in zip(sources, scales)]
    )
    head_out = (summed / pltpu.roll(total, back, 1)[:, 0:1]).astype(BF16)
    gath[i, z] = head_out
    att_ref[...] = head_out

    def copy3(n):
        to = lax.rem(z + n, 8)
        return pltpu.make_async_remote_copy(
            gath.at[i, z], gath.at[i, z], s3.at[n], r3.at[n], device_id=(to * 8 + i, x), device_id_type=MESH
        )

    def arrived3(n):
        slot = gath.at[i, lax.rem(z + 8 - n, 8)]
        return pltpu.make_async_remote_copy(
            slot, slot, s3.at[n], r3.at[n], device_id=(seq, x), device_id_type=MESH
        )

    for n in (4, 3, 5, 2, 6, 1, 7):
        copy3(n).start()
    estimate(1, 8, 24)
    for n in range(1, 8):
        arrived3(n).wait_recv()

    def copy4(n):
        to = lax.rem(i + n, 8)
        return pltpu.make_async_remote_copy(
            gath.at[i], gath.at[i], s4.at[n], r4.at[n], device_id=(z * 8 + to, x), device_id_type=MESH
        )

    def arrived4(n):
        slot = gath.at[lax.rem(i + 8 - n, 8)]
        return pltpu.make_async_remote_copy(
            slot, slot, s4.at[n], r4.at[n], device_id=(seq, x), device_id_type=MESH
        )

    for n in (4, 3, 5, 2, 6, 1, 7):
        copy4(n).start()
    estimate(1, 24, 32)
    finish_estimates(0)
    loads[5].wait()
    for n in range(1, 8):
        arrived4(n).wait_recv()

    for n in range(8):
        g32[pl.ds(n * 64, 64), :] = gath[n].astype(F32).reshape(64, 128)
    products = []
    for h in range(2):
        columns = []
        for g in range(8):
            columns.append(jnp.concatenate(
                [g32[pl.ds((2 * y_ + h) * 64 + g, 8, stride=8), :] for y_ in range(4)], axis=0
            ).astype(BF16))
        products.append(jnp.dot(
            jnp.concatenate(columns, axis=1), w[pl.ds(h * 1024, 1024), :], preferred_element_type=F32
        ))
    product = products[0] + products[1]
    for y_ in range(4):
        part[pl.ds(y_, 8, stride=4), :] = product[y_ * 8 : y_ * 8 + 8]

    def copy5(n):
        to = lax.rem(x + n, 4)
        return pltpu.make_async_remote_copy(
            part.at[pl.ds(pl.multiple_of(to * 8, 8), 8), :], recv5.at[n], s5.at[n], r5.at[n],
            device_id=(seq, to), device_id_type=MESH,
        )

    for n in (2, 1, 3):
        copy5(n).start()
    finish_estimates(1)
    result = part[pl.ds(pl.multiple_of(x * 8, 8), 8), :]
    for n in range(1, 4):
        copy5(n).wait_recv()
        result = result + recv5[n]
    lay_ref[...] = result.astype(BF16)

    for n in range(1, 8):
        copy1(n).wait_send()
        copy2(n).wait_send()
        copy3(n).wait_send()
        copy4(n).wait_send()
    for n in range(1, 4):
        copy5(n).wait_send()


def shards(queries, keys, values, codes, centroids, picks, block_len, out_weight):
    vmem = pltpu.VMEM
    dma = pltpu.SemaphoreType.DMA
    est, att, lay = pl.pallas_call(
        kernel,
        out_shape=(
            jax.ShapeDtypeStruct((2, 8, 32), F32),
            jax.ShapeDtypeStruct((8, 128), BF16),
            jax.ShapeDtypeStruct((8, 128), BF16),
        ),
        in_specs=[pl.BlockSpec(memory_space=pl.ANY)] * 8,
        out_specs=[pl.BlockSpec(memory_space=vmem)] * 3,
        scratch_shapes=[
            vmem((32, 2, 8, 128), BF16),
            vmem((8, 8, 128, 128), BF16),
            vmem((8, 8, 128, 128), BF16),
            vmem((32, 2, 32, 128), jnp.int32),
            vmem((2, 4, 32, 256), F32),
            vmem((64, 64), jnp.int32),
            vmem((8, 32), jnp.int32),
            vmem((2048, 128), BF16),
            vmem((2, 32, 128), F32),
            vmem((32, 128), F32),
            vmem((2, 256, 128), BF16),
            vmem((512, 128), F32),
            vmem((8, 9, 8, 128), BF16),
            vmem((8, 9, 8, 128), BF16),
            vmem((8, 2, 8, 128), BF16),
            vmem((8, 2, 8, 128), BF16),
            vmem((8, 8, 8, 128), BF16),
            vmem((512, 128), F32),
            vmem((32, 128), F32),
            vmem((4, 8, 128), F32),
            dma((6,)), dma((8,)), dma((8,)),
            dma((8,)), dma((8,)), dma((8,)), dma((8,)), dma((8,)), dma((8,)),
            dma((8,)), dma((8,)), dma((4,)), dma((4,)),
        ],
        compiler_params=pltpu.CompilerParams(
            collective_id=0, has_side_effects=True, vmem_limit_bytes=48 << 20
        ),
        name="decode",
    )(
        queries.reshape(32, 2, 8, 128),
        keys.reshape(8, 4, 2, 128, 128),
        values.reshape(8, 4, 2, 128, 128),
        codes,
        centroids,
        picks.reshape(64, 64),
        block_len.T,
        out_weight,
    )
    return est.transpose(2, 0, 1), att.reshape(1, 1, 1024), lay


def solution(mesh):
    placed = (
        P(None, "head", None),
        P(None, "head", "seq", None),
        P(None, "head", "seq", None),
        P(None, "head", None, "seq"),
        P("head", None, None, None),
        P(None, "head", None),
        P(None, "seq"),
        P("head", "seq"),
    )
    return jax.shard_map(
        shards,
        mesh=mesh,
        in_specs=placed,
        out_specs=(P(None, "head", "seq"), P("seq", "head", None), P("head", "seq")),
        check_vma=False,
    )
```

```python
import functools

import jax
import jax.numpy as jnp
from jax import lax
from jax.experimental import pallas as pl
from jax.experimental.pallas import tpu as pltpu
from jax.sharding import PartitionSpec as P

MESH = pl.DeviceIdType.MESH
NEG = -1e30
LIVE = -5e29
F32 = jnp.float32
BF16 = jnp.bfloat16
SCALE = 128 ** -0.5
GAP1 = 32
GAP2 = 32


def iota(shape, axis):
    return lax.broadcasted_iota(jnp.int32, shape, axis)


def lane_reduce(x, lane, op):
    for s in (1, 2, 4, 8):
        up = pltpu.roll(x, s, 1)
        down = pltpu.roll(x, 128 - s, 1)
        x = op(x, jnp.where((lane & s) != 0, up, down))
    return x


def lookup(rows, index):
    numbers = lax.GatherDimensionNumbers(
        offset_dims=(), collapsed_slice_dims=(1,), start_index_map=(1,),
        operand_batching_dims=(0,), start_indices_batching_dims=(0,),
    )
    return lax.gather(rows, index[..., None], numbers, (1, 1), mode=lax.GatherScatterMode.PROMISE_IN_BOUNDS)


def kernel(
    q_hbm, k_hbm, v_hbm, codes_hbm, cent_hbm, picks_hbm, len_hbm, w_hbm,
    est_ref, att_ref, lay_ref,
    q, k, v, codes, cent, picks, lens, w,
    bias, valid, q2, tab, acc, score, wide, send1, recv1, send2, recv2, gath, g32, part, recv5,
    in_sem, k_sem, v_sem, s1, r1, s2, r2, s4, r4, s5, r5,
):
    seq = lax.axis_index("seq")
    x = lax.axis_index("head")
    z = seq // 8
    i = lax.rem(seq, 8)

    def local(src, dst, n):
        return pltpu.make_async_copy(src, dst, in_sem.at[n])

    loads = [
        local(picks_hbm, picks, 0), local(len_hbm, lens, 1), local(q_hbm, q, 2),
        local(codes_hbm, codes, 3), local(cent_hbm, cent, 4), local(w_hbm, w, 5),
    ]
    kv = [
        (
            pltpu.make_async_copy(k_hbm.at[pl.ds(c * 8, 8)], k.at[pl.ds(c * 8, 8)], k_sem.at[c]),
            pltpu.make_async_copy(v_hbm.at[pl.ds(c * 8, 8)], v.at[pl.ds(c * 8, 8)], v_sem.at[c]),
        )
        for c in range(4)
    ]
    for c in loads[:3]:
        c.start()
    for c in kv:
        c[0].start()
    for c in kv:
        c[1].start()
    for c in loads[3:]:
        c.start()

    barrier = pltpu.get_barrier_semaphore()
    for n in range(1, 8):
        pl.semaphore_signal(barrier, inc=1, device_id=(z * 8 + lax.rem(i + n, 8), x), device_id_type=MESH)
        pl.semaphore_signal(barrier, inc=1, device_id=(lax.rem(z + n, 8) * 8 + i, x), device_id_type=MESH)
    for n in range(1, 4):
        pl.semaphore_signal(barrier, inc=1, device_id=(seq, lax.rem(x + n, 4)), device_id_type=MESH)

    lane = iota((8, 128), 1)
    block_of = iota((32, 128), 1) // 16

    loads[0].wait()
    loads[1].wait()
    spread = jnp.where(iota((8, 128), 1) // 16 == iota((8, 128), 0), 1.0, 0.0)
    len_rows = lens[...].astype(F32).T
    len_lane = jnp.dot(len_rows, spread, preferred_element_type=F32)
    place = (iota((32, 128), 1) & 15).astype(F32)
    is_valid = place < len_lane
    valid[...] = jnp.where(is_valid, 0.0, NEG)
    for h in range(2):
        near = picks[pl.ds(h, 32, stride=2), :] - seq * 8
        chosen = jnp.zeros((32, 128), F32)
        for j in range(8):
            hit = jnp.max(jnp.where(near == j, 1.0, 0.0), axis=1, keepdims=True)
            chosen = jnp.where(block_of == j, hit, chosen)
        bias[h] = jnp.where(is_valid & (chosen > 0.5), 0.0, NEG)

    loads[2].wait()
    for b in range(32):
        if b % 8 == 0:
            kv[b // 8][0].wait()
        both = lax.dot_general(
            q[b], k[b].reshape(256, 128), (((1,), (1,)), ((), ())), preferred_element_type=F32
        ) * SCALE
        score[b, 0] = both[:8, :128] + bias[0, b : b + 1, :]
        score[b, 1] = both[8:, 128:] + bias[1, b : b + 1, :]
    stats = [jnp.zeros((8, 128), F32)] * 8
    for c in range(4):
        tiles = [(b, h) for b in range(c * 8, c * 8 + 8) for h in range(2)]
        scores = [score[b, h] for b, h in tiles]
        tops = [jnp.max(s, axis=1, keepdims=True).astype(BF16).astype(F32) for s in scores]
        weights = [jnp.where(s > LIVE, jnp.exp(s - t), 0.0) for s, t in zip(scores, tops)]
        totals = [jnp.sum(e, axis=1, keepdims=True) for e in weights]
        for (b, h), top, weight, total in zip(tiles, tops, weights, totals):
            hi = weight.astype(BF16).astype(F32)
            wide[b, pl.ds(h * 8, 8), :] = hi
            wide[b, pl.ds(16 + h * 8, 8), :] = weight - hi
            j, n = (b % 4) * 2 + h, b // 4
            total_hi = total.astype(BF16).astype(F32)
            stat = jnp.where(lane == n, top, stats[j])
            stat = jnp.where(lane == 16 + n, total_hi, stat)
            stats[j] = jnp.where(lane == 32 + n, total - total_hi, stat)
    for j in range(8):
        send1[j, 8] = stats[j].astype(BF16)
    for b in range(32):
        if b % 8 == 0:
            kv[b // 8][1].wait()
        both = jnp.dot(
            wide[b].astype(BF16), jnp.concatenate([v[b, 0], v[b, 1]], axis=1), preferred_element_type=F32
        )
        for h in range(2):
            cols = slice(h * 128, h * 128 + 128)
            send1[(b % 4) * 2 + h, b // 4] = (
                both[h * 8 : h * 8 + 8, cols] + both[16 + h * 8 : 24 + h * 8, cols]
            ).astype(BF16)

    def copy1(n):
        j = lax.rem(i + n, 8)
        return pltpu.make_async_remote_copy(
            send1.at[j], recv1.at[n], s1.at[n], r1.at[n], device_id=(z * 8 + j, x), device_id_type=MESH
        )

    pl.semaphore_wait(barrier, 17)
    for n in (4, 3, 5, 2, 6, 1, 7):
        copy1(n).start()

    def table_one(h, m):
        row = iota((16, 256), 0) & 3
        pattern = jnp.broadcast_to(cent[h, 3, pl.ds(m, 1), :], (16, 256))
        for s in range(3):
            pattern = jnp.where(row == s, cent[h, s, pl.ds(m, 1), :], pattern)
        pattern = pattern * SCALE
        hi = pattern.astype(BF16)
        lo = (pattern - hi.astype(F32)).astype(BF16)
        own = jnp.where(iota((16, 128), 1) // 4 == m, 1.0, 0.0).astype(BF16)
        lhs = q2[h] * jnp.concatenate([own] * 16, axis=0)
        rhs = jnp.concatenate([hi] * 8 + [lo] * 8, axis=0)
        return jnp.dot(jnp.concatenate([lhs, lhs], axis=1), rhs, preferred_element_type=F32)

    def tables(low, high):
        def step(t, carry):
            h, m = t // 16, lax.rem(t, 16) * 2
            for u in range(2):
                tab[h, m + u] = table_one(h, m + u)
            return carry

        lax.fori_loop(low // 2, high // 2, step, 0)

    def lookups(low, high):
        def step(t, carry):
            h, b = t // 32, lax.rem(t, 32)
            sums = []
            at = pl.ds(pl.multiple_of(b * 8, 8), 8)
            for m in range(32):
                code = jnp.broadcast_to(codes[b, h, m : m + 1, :], (8, 128))
                index = code & 127
                first = lookup(tab[h, m, at, :128], index)
                second = lookup(tab[h, m, at, 128:], index)
                sums.append(jnp.where(code > 127, second, first))
            while len(sums) > 1:
                sums = [a + c for a, c in zip(sums[::2], sums[1::2])]
            acc[pl.ds(pl.multiple_of(t * 8, 8), 8), :] = sums[0]
            return carry

        lax.fori_loop(low, high, step, 0)

    def finish_estimates(h):
        rows = []
        for bb in range(4):
            base = (h * 32 + bb * 8) * 8
            off = valid[bb * 8 : bb * 8 + 8, :]
            parts = [acc[pl.ds(base + g, 8, stride=8), :] + off for g in range(8)]
            top = functools.reduce(jnp.maximum, parts)
            top = lane_reduce(top, lane, jnp.maximum)
            mass = functools.reduce(jnp.add, [jnp.where(off == 0.0, jnp.exp(a - top), 0.0) for a in parts])
            mass = lane_reduce(mass, lane, jnp.add)
            rows.append(top + jnp.log(mass))
        rows = jnp.concatenate(rows, axis=0)
        pick = jnp.where(iota((8, 128), 1) == iota((8, 128), 0) * 16, 1.0, 0.0)
        est_ref[h] = lax.dot_general(
            pick, rows, (((1,), (1,)), ((), ())), precision=lax.Precision.HIGHEST, preferred_element_type=F32
        )

    def merge(sources):
        stats = [a[8].astype(F32) for a in sources]
        top = functools.reduce(jnp.maximum, stats)
        scales = [jnp.exp(a - top) for a in stats]
        total = functools.reduce(
            jnp.add, [(pltpu.roll(a, 112, 1) + pltpu.roll(a, 96, 1)) * e for a, e in zip(stats, scales)]
        )
        sums = [
            functools.reduce(jnp.add, [e[:, n : n + 1] * a[n].astype(F32) for a, e in zip(sources, scales)])
            for n in range(8)
        ]
        return top, total, sums

    loads[3].wait()
    loads[4].wait()
    q2[0] = q[:, :8, :].reshape(256, 128)
    q2[1] = q[:, 8:, :].reshape(256, 128)
    tables(0, GAP1)

    for n in range(1, 8):
        copy1(n).wait_recv()
    top, total, sums = merge([send1.at[i]] + [recv1.at[n] for n in range(1, 8)])
    total_hi = total.astype(BF16).astype(F32)
    stat = jnp.where(lane < 8, top, jnp.where(
        lane < 32, pltpu.roll(total_hi, 16, 1), pltpu.roll(total - total_hi, 32, 1)))
    for n in range(8):
        send2[n] = sums[n].astype(BF16)
    send2[8] = stat.astype(BF16)

    def copy2(n):
        to = lax.rem(z + n, 8)
        return pltpu.make_async_remote_copy(
            send2, recv2.at[n], s2.at[n], r2.at[n], device_id=(to * 8 + i, x), device_id_type=MESH
        )

    for n in (4, 3, 5, 2, 6, 1, 7):
        copy2(n).start()
    tables(GAP1, 64)
    lookups(0, GAP2)

    for n in range(1, 8):
        copy2(n).wait_recv()
    top, total, sums = merge([send2] + [recv2.at[n] for n in range(1, 8)])
    for n in range(8):
        gath[i, n] = (sums[n] / total[:, n : n + 1]).astype(BF16)

    def copy4(n):
        to = lax.rem(i + n, 8)
        return pltpu.make_async_remote_copy(
            gath.at[i], gath.at[i], s4.at[n], r4.at[n], device_id=(z * 8 + to, x), device_id_type=MESH
        )

    def arrived4(n):
        slot = gath.at[lax.rem(i + 8 - n, 8)]
        return pltpu.make_async_remote_copy(
            slot, slot, s4.at[n], r4.at[n], device_id=(seq, x), device_id_type=MESH
        )

    for n in (4, 3, 5, 2, 6, 1, 7):
        copy4(n).start()
    att_ref[...] = gath[i, z]
    lookups(GAP2, 64)
    finish_estimates(0)
    loads[5].wait()
    for n in range(1, 8):
        arrived4(n).wait_recv()

    for n in range(8):
        g32[pl.ds(n * 64, 64), :] = gath[n].astype(F32).reshape(64, 128)
    products = []
    for h in range(2):
        columns = []
        for g in range(8):
            columns.append(jnp.concatenate(
                [g32[pl.ds((2 * y_ + h) * 64 + g, 8, stride=8), :] for y_ in range(4)], axis=0
            ).astype(BF16))
        products.append(jnp.dot(
            jnp.concatenate(columns, axis=1), w[pl.ds(h * 1024, 1024), :], preferred_element_type=F32
        ))
    product = products[0] + products[1]
    for y_ in range(4):
        part[pl.ds(y_, 8, stride=4), :] = product[y_ * 8 : y_ * 8 + 8]

    def copy5(n):
        to = lax.rem(x + n, 4)
        return pltpu.make_async_remote_copy(
            part.at[pl.ds(pl.multiple_of(to * 8, 8), 8), :], recv5.at[n], s5.at[n], r5.at[n],
            device_id=(seq, to), device_id_type=MESH,
        )

    for n in (2, 1, 3):
        copy5(n).start()
    finish_estimates(1)
    result = part[pl.ds(pl.multiple_of(x * 8, 8), 8), :]
    for n in range(1, 4):
        copy5(n).wait_recv()
        result = result + recv5[n]
    lay_ref[...] = result.astype(BF16)

    for n in range(1, 8):
        copy1(n).wait_send()
        copy2(n).wait_send()
        copy4(n).wait_send()
    for n in range(1, 4):
        copy5(n).wait_send()


def shards(queries, keys, values, codes, centroids, picks, block_len, out_weight):
    vmem = pltpu.VMEM
    dma = pltpu.SemaphoreType.DMA
    est, att, lay = pl.pallas_call(
        kernel,
        out_shape=(
            jax.ShapeDtypeStruct((2, 8, 32), F32),
            jax.ShapeDtypeStruct((8, 128), BF16),
            jax.ShapeDtypeStruct((8, 128), BF16),
        ),
        in_specs=[pl.BlockSpec(memory_space=pltpu.HBM)] * 8,
        out_specs=[pl.BlockSpec(memory_space=vmem)] * 3,
        scratch_shapes=[
            vmem((32, 16, 128), BF16),
            vmem((32, 2, 128, 128), BF16),
            vmem((32, 2, 128, 128), BF16),
            vmem((32, 2, 32, 128), jnp.int32),
            vmem((2, 4, 32, 256), F32),
            vmem((64, 64), jnp.int32),
            vmem((8, 32), jnp.int32),
            vmem((2048, 128), BF16),
            vmem((2, 32, 128), F32),
            vmem((32, 128), F32),
            vmem((2, 256, 128), BF16),
            vmem((2, 32, 256, 256), F32),
            vmem((512, 128), F32),
            vmem((32, 2, 8, 128), F32),
            vmem((32, 32, 128), F32),
            vmem((8, 9, 8, 128), BF16),
            vmem((8, 9, 8, 128), BF16),
            vmem((9, 8, 128), BF16),
            vmem((8, 9, 8, 128), BF16),
            vmem((8, 8, 8, 128), BF16),
            vmem((512, 128), F32),
            vmem((32, 128), F32),
            vmem((4, 8, 128), F32),
            dma((6,)), dma((4,)), dma((4,)),
            dma((8,)), dma((8,)), dma((8,)), dma((8,)), dma((8,)), dma((8,)), dma((4,)), dma((4,)),
        ],
        compiler_params=pltpu.CompilerParams(
            collective_id=0, has_side_effects=True, vmem_limit_bytes=67_043_328
        ),
        name="decode",
    )(
        queries,
        keys,
        values,
        codes,
        centroids,
        picks.reshape(64, 64),
        block_len.T,
        out_weight,
    )
    return est.transpose(2, 0, 1), att.reshape(1, 1, 1024), lay


def solution(mesh):
    placed = (
        P(None, "head", None),
        P(None, "head", "seq", None),
        P(None, "head", "seq", None),
        P(None, "head", None, "seq"),
        P("head", None, None, None),
        P(None, "head", None),
        P(None, "seq"),
        P("head", "seq"),
    )
    return jax.shard_map(
        shards,
        mesh=mesh,
        in_specs=placed,
        out_specs=(P(None, "head", "seq"), P("seq", "head", None), P("head", "seq")),
        check_vma=False,
    )
```

```python
import functools

import jax
import jax.numpy as jnp
from jax import lax
from jax.experimental import pallas as pl
from jax.experimental.pallas import tpu as pltpu
from jax.sharding import PartitionSpec as P

MESH = pl.DeviceIdType.MESH
NEG = -1e30
LIVE = -5e29
F32 = jnp.float32
BF16 = jnp.bfloat16
SCALE = 128 ** -0.5
STEP = 1280.0
GAP1 = 16
GAP2 = 32


def iota(shape, axis):
    return lax.broadcasted_iota(jnp.int32, shape, axis)


def lane_reduce(x, lane, op):
    for s in (1, 2, 4, 8):
        up = pltpu.roll(x, s, 1)
        down = pltpu.roll(x, 128 - s, 1)
        x = op(x, jnp.where((lane & s) != 0, up, down))
    return x


def lookup(rows, index):
    numbers = lax.GatherDimensionNumbers(
        offset_dims=(), collapsed_slice_dims=(1,), start_index_map=(1,),
        operand_batching_dims=(0,), start_indices_batching_dims=(0,),
    )
    return lax.gather(rows, index[..., None], numbers, (1, 1), mode=lax.GatherScatterMode.PROMISE_IN_BOUNDS)


def kernel(
    q_hbm, k_hbm, v_hbm, codes_hbm, cent_hbm, picks_hbm, len_hbm, w_hbm,
    est_ref, att_ref, lay_ref,
    q, k, v, codes, cent, picks, lens, w,
    bias, valid, q2, tab, acc, score, wide, send1, recv1, send2, recv2, gath, g32, part, recv5,
    in_sem, k_sem, v_sem, s1, r1, s2, r2, s4, r4, s5, r5,
):
    seq = lax.axis_index("seq")
    x = lax.axis_index("head")
    z = seq // 8
    i = lax.rem(seq, 8)

    def local(src, dst, n):
        return pltpu.make_async_copy(src, dst, in_sem.at[n])

    loads = [
        local(picks_hbm, picks, 0), local(len_hbm, lens, 1), local(q_hbm, q, 2),
        local(codes_hbm, codes, 3), local(cent_hbm, cent, 4), local(w_hbm, w, 5),
    ]
    kv = [
        (
            pltpu.make_async_copy(k_hbm.at[pl.ds(c * 8, 8)], k.at[pl.ds(c * 8, 8)], k_sem.at[c]),
            pltpu.make_async_copy(v_hbm.at[pl.ds(c * 8, 8)], v.at[pl.ds(c * 8, 8)], v_sem.at[c]),
        )
        for c in range(4)
    ]
    for c in loads[:3]:
        c.start()
    for c in kv:
        c[0].start()
    for c in kv:
        c[1].start()
    for c in loads[3:]:
        c.start()

    barrier = pltpu.get_barrier_semaphore()
    for n in range(1, 8):
        pl.semaphore_signal(barrier, inc=1, device_id=(z * 8 + lax.rem(i + n, 8), x), device_id_type=MESH)
        pl.semaphore_signal(barrier, inc=1, device_id=(lax.rem(z + n, 8) * 8 + i, x), device_id_type=MESH)
    for n in range(1, 4):
        pl.semaphore_signal(barrier, inc=1, device_id=(seq, lax.rem(x + n, 4)), device_id_type=MESH)

    lane = iota((8, 128), 1)
    block_of = iota((32, 128), 1) // 16

    loads[0].wait()
    loads[1].wait()
    spread = jnp.where(iota((8, 128), 1) // 16 == iota((8, 128), 0), 1.0, 0.0)
    len_rows = lens[...].astype(F32).T
    len_lane = jnp.dot(len_rows, spread, preferred_element_type=F32)
    place = (iota((32, 128), 1) & 15).astype(F32)
    is_valid = place < len_lane
    valid[...] = jnp.where(is_valid, 0.0, NEG)
    for h in range(2):
        near = picks[pl.ds(h, 32, stride=2), :] - seq * 8
        chosen = jnp.zeros((32, 128), F32)
        for j in range(8):
            hit = jnp.max(jnp.where(near == j, 1.0, 0.0), axis=1, keepdims=True)
            chosen = jnp.where(block_of == j, hit, chosen)
        bias[h] = jnp.where(is_valid & (chosen > 0.5), 0.0, NEG)

    loads[2].wait()
    for b in range(32):
        if b % 8 == 0:
            kv[b // 8][0].wait()
        both = lax.dot_general(
            q[b], k[b].reshape(256, 128), (((1,), (1,)), ((), ())), preferred_element_type=F32
        ) * SCALE
        score[b, 0] = both[:8, :128] + bias[0, b : b + 1, :]
        score[b, 1] = both[8:, 128:] + bias[1, b : b + 1, :]
    stats = [jnp.zeros((8, 128), F32)] * 8
    for c in range(4):
        tiles = [(b, h) for b in range(c * 8, c * 8 + 8) for h in range(2)]
        scores = [score[b, h] for b, h in tiles]
        tops = [jnp.max(s, axis=1, keepdims=True).astype(BF16).astype(F32) for s in scores]
        weights = [jnp.where(s > LIVE, jnp.exp(s - t), 0.0) for s, t in zip(scores, tops)]
        totals = [jnp.sum(e, axis=1, keepdims=True) for e in weights]
        for (b, h), top, weight, total in zip(tiles, tops, weights, totals):
            hi = weight.astype(BF16).astype(F32)
            wide[b, pl.ds(h * 8, 8), :] = hi
            wide[b, pl.ds(16 + h * 8, 8), :] = weight - hi
            j, n = (b % 4) * 2 + h, b // 4
            total_hi = total.astype(BF16).astype(F32)
            stat = jnp.where(lane == n, top, stats[j])
            stat = jnp.where(lane == 16 + n, total_hi, stat)
            stats[j] = jnp.where(lane == 32 + n, total - total_hi, stat)
    for j in range(8):
        send1[j, 8] = stats[j].astype(BF16)
    for b in range(32):
        if b % 8 == 0:
            kv[b // 8][1].wait()
        both = jnp.dot(
            wide[b].astype(BF16), jnp.concatenate([v[b, 0], v[b, 1]], axis=1), preferred_element_type=F32
        )
        for h in range(2):
            cols = slice(h * 128, h * 128 + 128)
            send1[(b % 4) * 2 + h, b // 4] = (
                both[h * 8 : h * 8 + 8, cols] + both[16 + h * 8 : 24 + h * 8, cols]
            ).astype(BF16)

    def copy1(n):
        j = lax.rem(i + n, 8)
        return pltpu.make_async_remote_copy(
            send1.at[j], recv1.at[n], s1.at[n], r1.at[n], device_id=(z * 8 + j, x), device_id_type=MESH
        )

    pl.semaphore_wait(barrier, 17)
    for n in (4, 3, 5, 2, 6, 1, 7):
        copy1(n).start()

    sub = iota((8, 128), 0)

    def tables(low, high):
        def step(t, carry):
            h, m = t // 16, lax.rem(t, 16)
            row = iota((16, 256), 0)
            tiles = []
            for at in (m, m + 16):
                pattern = jnp.broadcast_to(cent[h, 3, pl.ds(at, 1), :], (16, 256))
                for s in range(3):
                    pattern = jnp.where((row & 3) == s, cent[h, s, pl.ds(at, 1), :], pattern)
                pattern = pattern * (SCALE * STEP)
                hi = pattern.astype(BF16)
                tiles.append((hi, (pattern - hi.astype(F32)).astype(BF16)))
            rhs = jnp.concatenate(
                [tiles[0][0]] * 4 + [tiles[1][0]] * 4 + [tiles[0][1]] * 4 + [tiles[1][1]] * 4, axis=0
            )
            target = jnp.where((row[:, :128] & 7) < 4, m, m + 16)
            own = jnp.where(iota((16, 128), 1) // 4 == target, 1.0, 0.0).astype(BF16)
            lhs = q2[h] * jnp.concatenate([own] * 32, axis=0)
            table = jnp.dot(jnp.concatenate([lhs, lhs], axis=1), rhs, preferred_element_type=F32)
            for b in range(32):
                first = (table[b * 16 : b * 16 + 8] + 32768.5).astype(jnp.int32)
                second = (table[b * 16 + 8 : b * 16 + 16] + 32768.5).astype(jnp.int32)
                tab[h, m, b] = first | (second << 16)
            return carry

        lax.fori_loop(low, high, step, 0)

    def lookups(low, high):
        def step(t, carry):
            h, b = t // 32, lax.rem(t, 32)
            firsts, seconds = [], []
            for m in range(16):
                code = jnp.where(sub < 4, codes[b, h, m : m + 1, :], codes[b, h, m + 16 : m + 17, :])
                index = code & 127
                word = jnp.where(
                    code > 127, lookup(tab[h, m, b, :, 128:], index), lookup(tab[h, m, b, :, :128], index)
                )
                firsts.append(word & 65535)
                seconds.append(lax.shift_right_logical(word, 16))
            at = pl.multiple_of(t * 16, 16)
            for sums, rows in ((firsts, pl.ds(at, 8)), (seconds, pl.ds(at + 8, 8))):
                while len(sums) > 1:
                    sums = [a + c for a, c in zip(sums[::2], sums[1::2])]
                acc[rows, :] = sums[0]
            return carry

        lax.fori_loop(low, high, step, 0)

    def finish_estimates(h):
        rows = []
        for bb in range(4):
            base = (h * 32 + bb * 8) * 16
            off = valid[bb * 8 : bb * 8 + 8, :]
            parts = []
            for g in range(8):
                at = base + g // 4 * 8 + g % 4
                total = acc[pl.ds(at, 8, stride=16), :] + acc[pl.ds(at + 4, 8, stride=16), :]
                parts.append((total - 32 * 32768).astype(F32) * (1.0 / STEP) + off)
            top = functools.reduce(jnp.maximum, parts)
            top = lane_reduce(top, lane, jnp.maximum)
            mass = functools.reduce(jnp.add, [jnp.where(off == 0.0, jnp.exp(a - top), 0.0) for a in parts])
            mass = lane_reduce(mass, lane, jnp.add)
            rows.append(top + jnp.log(mass))
        rows = jnp.concatenate(rows, axis=0)
        pick = jnp.where(iota((8, 128), 1) == iota((8, 128), 0) * 16, 1.0, 0.0)
        est_ref[h] = lax.dot_general(
            pick, rows, (((1,), (1,)), ((), ())), precision=lax.Precision.HIGHEST, preferred_element_type=F32
        )

    def merge(sources):
        stats = [a[8].astype(F32) for a in sources]
        top = functools.reduce(jnp.maximum, stats)
        scales = [jnp.exp(a - top) for a in stats]
        total = functools.reduce(
            jnp.add, [(pltpu.roll(a, 112, 1) + pltpu.roll(a, 96, 1)) * e for a, e in zip(stats, scales)]
        )
        sums = [
            functools.reduce(jnp.add, [e[:, n : n + 1] * a[n].astype(F32) for a, e in zip(sources, scales)])
            for n in range(8)
        ]
        return top, total, sums

    loads[3].wait()
    loads[4].wait()
    low_half = iota((32, 8, 128), 1) < 4
    for h in range(2):
        own = q[...].astype(F32)[:, h * 8 : h * 8 + 8, :]
        swapped = pltpu.roll(own, 4, 1)
        both = jnp.concatenate(
            [jnp.where(low_half, own, swapped), jnp.where(low_half, swapped, own)], axis=1
        )
        q2[h] = both.astype(BF16).reshape(512, 128)
    tables(0, GAP1)

    for n in range(1, 8):
        copy1(n).wait_recv()
    top, total, sums = merge([send1.at[i]] + [recv1.at[n] for n in range(1, 8)])
    total_hi = total.astype(BF16).astype(F32)
    stat = jnp.where(lane < 8, top, jnp.where(
        lane < 32, pltpu.roll(total_hi, 16, 1), pltpu.roll(total - total_hi, 32, 1)))
    for n in range(8):
        send2[n] = sums[n].astype(BF16)
    send2[8] = stat.astype(BF16)

    def copy2(n):
        to = lax.rem(z + n, 8)
        return pltpu.make_async_remote_copy(
            send2, recv2.at[n], s2.at[n], r2.at[n], device_id=(to * 8 + i, x), device_id_type=MESH
        )

    for n in (4, 3, 5, 2, 6, 1, 7):
        copy2(n).start()
    tables(GAP1, 32)
    lookups(0, GAP2)

    for n in range(1, 8):
        copy2(n).wait_recv()
    top, total, sums = merge([send2] + [recv2.at[n] for n in range(1, 8)])
    for n in range(8):
        gath[i, n] = (sums[n] / total[:, n : n + 1]).astype(BF16)

    def copy4(n):
        to = lax.rem(i + n, 8)
        return pltpu.make_async_remote_copy(
            gath.at[i], gath.at[i], s4.at[n], r4.at[n], device_id=(z * 8 + to, x), device_id_type=MESH
        )

    def arrived4(n):
        slot = gath.at[lax.rem(i + 8 - n, 8)]
        return pltpu.make_async_remote_copy(
            slot, slot, s4.at[n], r4.at[n], device_id=(seq, x), device_id_type=MESH
        )

    for n in (4, 3, 5, 2, 6, 1, 7):
        copy4(n).start()
    att_ref[...] = gath[i, z]
    lookups(GAP2, 64)
    finish_estimates(0)
    loads[5].wait()
    for n in range(1, 8):
        arrived4(n).wait_recv()

    for n in range(8):
        g32[pl.ds(n * 64, 64), :] = gath[n].astype(F32).reshape(64, 128)
    products = []
    for h in range(2):
        columns = []
        for g in range(8):
            columns.append(jnp.concatenate(
                [g32[pl.ds((2 * y_ + h) * 64 + g, 8, stride=8), :] for y_ in range(4)], axis=0
            ).astype(BF16))
        products.append(jnp.dot(
            jnp.concatenate(columns, axis=1), w[pl.ds(h * 1024, 1024), :], preferred_element_type=F32
        ))
    product = products[0] + products[1]
    for y_ in range(4):
        part[pl.ds(y_, 8, stride=4), :] = product[y_ * 8 : y_ * 8 + 8]

    def copy5(n):
        to = lax.rem(x + n, 4)
        return pltpu.make_async_remote_copy(
            part.at[pl.ds(pl.multiple_of(to * 8, 8), 8), :], recv5.at[n], s5.at[n], r5.at[n],
            device_id=(seq, to), device_id_type=MESH,
        )

    for n in (2, 1, 3):
        copy5(n).start()
    finish_estimates(1)
    result = part[pl.ds(pl.multiple_of(x * 8, 8), 8), :]
    for n in range(1, 4):
        copy5(n).wait_recv()
        result = result + recv5[n]
    lay_ref[...] = result.astype(BF16)

    for n in range(1, 8):
        copy1(n).wait_send()
        copy2(n).wait_send()
        copy4(n).wait_send()
    for n in range(1, 4):
        copy5(n).wait_send()


def shards(queries, keys, values, codes, centroids, picks, block_len, out_weight):
    vmem = pltpu.VMEM
    dma = pltpu.SemaphoreType.DMA
    est, att, lay = pl.pallas_call(
        kernel,
        out_shape=(
            jax.ShapeDtypeStruct((2, 8, 32), F32),
            jax.ShapeDtypeStruct((8, 128), BF16),
            jax.ShapeDtypeStruct((8, 128), BF16),
        ),
        in_specs=[pl.BlockSpec(memory_space=pltpu.HBM)] * 8,
        out_specs=[pl.BlockSpec(memory_space=vmem)] * 3,
        scratch_shapes=[
            vmem((32, 16, 128), BF16),
            vmem((32, 2, 128, 128), BF16),
            vmem((32, 2, 128, 128), BF16),
            vmem((32, 2, 32, 128), jnp.int32),
            vmem((2, 4, 32, 256), F32),
            vmem((64, 64), jnp.int32),
            vmem((8, 32), jnp.int32),
            vmem((2048, 128), BF16),
            vmem((2, 32, 128), F32),
            vmem((32, 128), F32),
            vmem((2, 512, 128), BF16),
            vmem((2, 16, 32, 8, 256), jnp.int32),
            vmem((1024, 128), jnp.int32),
            vmem((32, 2, 8, 128), F32),
            vmem((32, 32, 128), F32),
            vmem((8, 9, 8, 128), BF16),
            vmem((8, 9, 8, 128), BF16),
            vmem((9, 8, 128), BF16),
            vmem((8, 9, 8, 128), BF16),
            vmem((8, 8, 8, 128), BF16),
            vmem((512, 128), F32),
            vmem((32, 128), F32),
            vmem((4, 8, 128), F32),
            dma((6,)), dma((4,)), dma((4,)),
            dma((8,)), dma((8,)), dma((8,)), dma((8,)), dma((8,)), dma((8,)), dma((4,)), dma((4,)),
        ],
        compiler_params=pltpu.CompilerParams(
            collective_id=0, has_side_effects=True, vmem_limit_bytes=67_043_328
        ),
        name="decode",
    )(
        queries,
        keys,
        values,
        codes,
        centroids,
        picks.reshape(64, 64),
        block_len.T,
        out_weight,
    )
    return est.transpose(2, 0, 1), att.reshape(1, 1, 1024), lay


def solution(mesh):
    placed = (
        P(None, "head", None),
        P(None, "head", "seq", None),
        P(None, "head", "seq", None),
        P(None, "head", None, "seq"),
        P("head", None, None, None),
        P(None, "head", None),
        P(None, "seq"),
        P("head", "seq"),
    )
    return jax.shard_map(
        shards,
        mesh=mesh,
        in_specs=placed,
        out_specs=(P(None, "head", "seq"), P("seq", "head", None), P("head", "seq")),
        check_vma=False,
    )
```
